32 devices in a mesh: tile: 8 (over z, x), trace: 4 (over y, core).
Axes of the slice: x: 2, y: 2, z: 4, core: 2. Of those that a mesh axis runs over, the one named last changes fastest.
Arguments:
- traces: bfloat16 [4, 128, 32, 256], P('trace', 'tile'), may hold values from -6 to 6
- taps: bfloat16 [2, 65], replicated, may hold values from -0.75 to 0.75
- aperture: int32 [4, 8, 128], P('trace'), may hold values from 0 to 127, as said below
- counts: int32 [4, 8], P('trace'), may hold values from 32 to 128, as said below
- time_weights: bfloat16 [4, 8, 128, 128, 256], P('trace', 'tile'), may hold values from -0.375 to 0.375
- amplitudes: bfloat16 [4, 8, 128, 2, 32, 256], P('trace', 'tile'), may hold values from -0.0625 to 0.0625
Outputs:
- image: float32 [8, 128, 256], P('tile', 'trace')
The draws below stay inside these ranges and needn't reach their ends.
Inputs may be any that keep to these rules, and one draw needn't show every extreme that they name: `aperture`: entries of one list are distinct ids of the subset's blocks; they come in runs of 16 consecutive entries whose ids share the owner index id // 16, and no owner index appears in more than one run of a list. `counts`: some list uses all 128 entries and some uses 128 // 4.
All inputs are finite; a program needn't handle non-finite values.
Results may differ from the reference program's by a relative error of at most 0.0041.
Values may be sent and summed in bfloat16 or wider, within the bound.
A program may use at most 64 MiB of HBM per device.

```python
import jax
import jax.numpy as jnp
from jax import lax

NS = 256
NTAU = 128
TAPS = 65
TRACE_BLK = 32
BLK_DEV = 16
SLOTS = 128
COLS = 256
HALF = 32
TILES = 8
SUBSETS = 4
BLOCKS = 128
CAP = 16


def draw_counts(key, part):
    key_values, key_upper, key_lower = jax.random.split(key, 3)
    entries = SUBSETS * TILES
    values = jax.random.randint(key_values, (entries,), SLOTS // 4, SLOTS + 1)
    upper = jax.random.randint(key_upper, (), 0, entries)
    lower = (upper + 1 + jax.random.randint(key_lower, (), 0, entries - 1)) % entries
    values = values.at[upper].set(SLOTS).at[lower].set(SLOTS // 4)
    return values.reshape(SUBSETS, TILES).astype(jnp.int32)


def permute_tiles(subkey):
    return jax.random.permutation(subkey, TILES)


def permute_blocks(subkey):
    return jax.random.permutation(subkey, BLK_DEV)


def draw_aperture(key, part):
    list_count = SUBSETS * TILES
    run_count = SLOTS // CAP
    owner_keys = jax.random.split(jax.random.fold_in(key, 11), list_count)
    owners = jax.vmap(permute_tiles)(owner_keys)[:, :run_count]
    within_keys = jax.random.split(jax.random.fold_in(key, 23), list_count * run_count)
    within = jax.vmap(permute_blocks)(within_keys)[:, :CAP].reshape(list_count, SLOTS)
    slot_owner = jnp.repeat(owners, CAP, axis=1)
    return (slot_owner * BLK_DEV + within).reshape(SUBSETS, TILES, SLOTS).astype(jnp.int32)


def shard_levels(rng, extent, shards, smallest, top_value):
    def one(axis_at, shards_of):
        steps = jax.random.uniform(jax.random.fold_in(jax.random.fold_in(rng, 6), axis_at), (shards_of,), jnp.float32, smallest / len(shards), top_value / len(shards))
        return jnp.repeat(jnp.exp(steps), extent[axis_at] // shards_of).reshape((-1,) + (1,) * (len(extent) - axis_at - 1))

    factor_of = one(*shards[0])
    for cut in shards[1:]:
        factor_of = factor_of * one(*cut)
    return factor_of


def normal_values(rng, dims, scale, bound, shards=(), dtype=jnp.bfloat16):
    drawn = jax.random.normal(rng, dims, jnp.float32) * scale
    if len(shards) > 0:
        drawn = shard_levels(rng, dims, shards, -0.22, 0.18) * drawn
    return jnp.clip(drawn, min=-bound, max=bound).astype(dtype)


def setup_inputs(seed: int = 0) -> dict:
    streams_of = jax.random.split(jax.random.key(seed), 7)
    return {
        "traces": normal_values(streams_of[0], (SUBSETS, BLOCKS, TRACE_BLK, NS), 1.0, 6.0, ((0, 4), (1, 8))),
        "taps": normal_values(streams_of[1], (2, TAPS), TAPS ** -0.5, 0.75),
        "aperture": draw_aperture(jax.random.fold_in(streams_of[6], 71), 0),
        "counts": draw_counts(jax.random.fold_in(streams_of[6], 71), 0),
        "time_weights": normal_values(streams_of[4], (SUBSETS, TILES, SLOTS, NTAU, NS), NS ** -0.5, 0.375, ((0, 4), (1, 8))),
        "amplitudes": normal_values(streams_of[5], (SUBSETS, TILES, SLOTS, 2, TRACE_BLK, COLS), (2 * TRACE_BLK * SLOTS) ** -0.5, 0.0625, ((0, 4), (1, 8))),
    }


def filter_matrix(taps):
    offset = jnp.arange(NS)[:, None] - jnp.arange(NS)[None, :] + HALF
    inside = (offset >= 0) & (offset < TAPS)
    picked = jnp.take(taps, jnp.clip(offset, 0, TAPS - 1).astype(jnp.int32), axis=1)
    return jnp.where(inside[None], picked, jnp.zeros_like(picked))


def reference(traces, taps, aperture, counts, time_weights, amplitudes):
    operator = filter_matrix(taps).astype(jnp.float32)
    image = jnp.zeros((TILES, NTAU, COLS), jnp.float32)
    for subset in range(SUBSETS):
        filtered = jnp.einsum('cnm,kbm->kcbn', operator, traces[subset].astype(jnp.float32)).astype(jnp.bfloat16)

        def one_tile(packed):
            listing, filled, weights, spread = packed
            blocks = jnp.take(filtered, listing, axis=0).astype(jnp.float32)
            alive = (jnp.arange(SLOTS) < filled).astype(jnp.float32)
            interp = jnp.einsum('stn,scbn->scbt', weights.astype(jnp.float32), blocks) * alive[:, None, None, None]
            interp = lax.optimization_barrier(interp.astype(jnp.bfloat16)).astype(jnp.float32)
            return jnp.einsum('scbt,scbp->tp', interp, spread.astype(jnp.float32))

        image = image + lax.map(one_tile, (aperture[subset], counts[subset], time_weights[subset], amplitudes[subset]))
    return image
```

```python
import functools

import jax
import jax.numpy as jnp
from jax import lax
from jax.experimental import pallas as pl
from jax.experimental.pallas import tpu as pltpu
from jax.sharding import PartitionSpec as P

group_slots = 8
lane_group = 4
halves = 2
MESH = pl.DeviceIdType.MESH


def migrate_kernel(
    rows_z,
    subsets,
    half_taps,
    inv_ref,
    alive_ref,
    band_ref,
    traces_ref,
    weights_ref,
    spread_ref,
    out_ref,
    gathered,
    weights,
    spread,
    operator,
    filtered,
    total,
    parts,
    recv_sem,
    send_z_sem,
    send_x_sem,
    load_sem,
    part_send_sem,
    part_recv_sem,
):
    tile = lax.axis_index("tile")
    subset = lax.axis_index("trace")
    z = tile // 2
    x = tile % 2
    other = 1 - x
    samples = operator.shape[1]
    chunk_rows = gathered.shape[2]
    block_rows = spread.shape[2]
    chunk_blocks = chunk_rows // block_rows
    block_count = chunk_blocks * halves
    group_lanes = lane_group * block_rows

    load_own = pltpu.make_async_copy(traces_ref, gathered.at[tile], load_sem.at[0])
    load_weights = pltpu.make_async_copy(weights_ref, weights, load_sem.at[1])
    load_spread = pltpu.make_async_copy(spread_ref, spread, load_sem.at[2])

    barrier = pltpu.get_barrier_semaphore()

    @pl.when(z > 0)
    def _():
        pl.semaphore_signal(barrier, inc=1, device_id=(tile - 2, subset), device_id_type=MESH)

    @pl.when(z < rows_z - 1)
    def _():
        pl.semaphore_signal(barrier, inc=1, device_id=(tile + 2, subset), device_id_type=MESH)

    pl.semaphore_signal(barrier, inc=1, device_id=(z * 2 + other, subset), device_id_type=MESH)
    for step in range(1, subsets):
        pl.semaphore_signal(
            barrier, inc=1, device_id=(tile, (subset + step) % subsets), device_id_type=MESH
        )
    load_own.start()
    load_weights.start()
    load_spread.start()
    inner = jnp.where((z > 0) & (z < rows_z - 1), 1, 0)
    pl.semaphore_wait(barrier, subsets + 1 + inner)

    def source(origin_z, half, own):
        if own:
            return traces_ref.at[half]
        return gathered.at[origin_z * 2 + x, half]

    def send_z(origin_z, half, up, own=False):
        return pltpu.make_async_remote_copy(
            src_ref=source(origin_z, half, own),
            dst_ref=gathered.at[origin_z * 2 + x, half],
            send_sem=send_z_sem.at[up, origin_z, half],
            recv_sem=recv_sem.at[origin_z * 2 + x, half],
            device_id=(tile + 4 * up - 2, subset),
            device_id_type=MESH,
        )

    def send_x(origin_z, half, own=False):
        return pltpu.make_async_remote_copy(
            src_ref=source(origin_z, half, own),
            dst_ref=gathered.at[origin_z * 2 + x, half],
            send_sem=send_x_sem.at[origin_z, half],
            recv_sem=recv_sem.at[origin_z * 2 + x, half],
            device_id=(z * 2 + other, subset),
            device_id_type=MESH,
        )

    def wait_arrival(origin, half):
        pltpu.make_async_remote_copy(
            src_ref=gathered.at[origin, half],
            dst_ref=gathered.at[origin, half],
            send_sem=send_x_sem.at[0, 0],
            recv_sem=recv_sem.at[origin, half],
            device_id=(z * 2 + other, subset),
            device_id_type=MESH,
        ).wait_recv()

    for half in range(halves):

        @pl.when(z < rows_z - 1)
        def _():
            send_z(z, half, 1, True).start()

        @pl.when(z > 0)
        def _():
            send_z(z, half, 0, True).start()

        send_x(z, half, True).start()

    row = lax.broadcasted_iota(jnp.int32, (samples, samples), 0)
    gap = lax.broadcasted_iota(jnp.int32, (samples, samples), 1) - row
    inside = (gap <= half_taps) & (gap >= -half_taps)
    for channel in range(2):
        band = jnp.broadcast_to(band_ref[channel : channel + 1, :], (samples, samples))
        shift = 1
        while shift < samples:
            band = jnp.where((row // shift) % 2 == 1, pltpu.roll(band, shift, 1), band)
            shift *= 2
        operator[channel * samples : (channel + 1) * samples, :] = jnp.where(
            inside, band, 0.0
        ).astype(operator.dtype)
    total[...] = jnp.zeros_like(total)

    lanes = lax.broadcasted_iota(jnp.int32, (1, 2 * group_lanes), 1)
    member = (lanes // block_rows) % lane_group

    def compute(origin, half):
        filtered[...] = lax.dot_general(
            operator[...],
            gathered[origin, half],
            (((1,), (1,)), ((), ())),
            preferred_element_type=jnp.float32,
        ).astype(filtered.dtype)
        taus = weights.shape[1]
        for group in range(chunk_blocks // lane_group):
            first = group * group_lanes
            blocks = jnp.concatenate(
                [
                    filtered[0:samples, first : first + group_lanes],
                    filtered[samples : 2 * samples, first : first + group_lanes],
                ],
                axis=1,
            )
            base = origin * block_count + half * chunk_blocks + group * lane_group
            slots = [inv_ref[base + index] for index in range(lane_group)]
            stacked = jnp.concatenate([weights[slot] for slot in slots], axis=0)
            product = jnp.dot(stacked, blocks, preferred_element_type=jnp.float32)
            interp = product[0:taus]
            alive = jnp.full((1, 2 * group_lanes), alive_ref[base], jnp.float32)
            for index in range(1, lane_group):
                here = member == index
                interp = jnp.where(here, product[index * taus : (index + 1) * taus], interp)
                alive = jnp.where(here, alive_ref[base + index], alive)
            interp = (interp * alive).astype(jnp.bfloat16)
            columns = jnp.concatenate(
                [spread[slot, channel] for channel in range(2) for slot in slots], axis=0
            )
            total[...] += jnp.dot(interp, columns, preferred_element_type=jnp.float32)

    load_own.wait()
    load_weights.wait()
    load_spread.wait()

    def own_chunk(half, carry):
        compute(tile, half)
        return carry

    lax.fori_loop(0, halves, own_chunk, 0)

    for distance in range(1, rows_z + 1):
        for half in range(halves):
            for up in (1, 0):
                origin_z = z - distance if up else z + distance

                @pl.when((origin_z >= 0) & (origin_z < rows_z))
                def _():
                    wait_arrival(origin_z * 2 + x, half)

                    @pl.when((z > 0) & (z < rows_z - 1))
                    def _():
                        send_z(origin_z, half, up).start()

                    send_x(origin_z, half).start()

        def column_chunk(event, carry):
            half = event // 2
            up = event % 2
            near = z - distance * (2 * up - 1)
            far = z - (distance - 1) * (2 * up - 1)

            @pl.when((near >= 0) & (near < rows_z))
            def _():
                compute(near * 2 + x, half)

            if distance > 1:
                wanted = (far >= 0) & (far < rows_z)
            else:
                wanted = up == 1

            @pl.when(wanted)
            def _():
                wait_arrival(far * 2 + other, half)
                compute(far * 2 + other, half)

            return carry

        lax.fori_loop(0, 2 * halves, column_chunk, 0)

    share = out_ref.shape[0]
    sends = []
    for step in range(1, subsets):
        peer = (subset + step) % subsets
        copy = pltpu.make_async_remote_copy(
            src_ref=total.at[pl.ds(pl.multiple_of(peer * share, share), share)],
            dst_ref=parts.at[step - 1],
            send_sem=part_send_sem.at[step - 1],
            recv_sem=part_recv_sem.at[step - 1],
            device_id=(tile, peer),
            device_id_type=MESH,
        )
        copy.start()
        sends.append(copy)
    result = total[pl.ds(pl.multiple_of(subset * share, share), share), :]
    for step in range(1, subsets):
        sends[step - 1].wait_recv()
        result = result + parts[step - 1]
    out_ref[...] = result
    for copy in sends:
        copy.wait_send()

    for half in range(halves):

        @pl.when(z < rows_z - 1)
        def _():
            send_z(z, half, 1, True).wait_send()

        @pl.when(z > 0)
        def _():
            send_z(z, half, 0, True).wait_send()

        send_x(z, half, True).wait_send()
        for distance in range(1, rows_z):
            for up in (1, 0):
                origin_z = z - distance if up else z + distance

                @pl.when((origin_z >= 0) & (origin_z < rows_z))
                def _():
                    @pl.when((z > 0) & (z < rows_z - 1))
                    def _():
                        send_z(origin_z, half, up).wait_send()

                    send_x(origin_z, half).wait_send()


def gather_per_device(traces, taps, aperture, counts, time_weights, amplitudes):
    tiles = lax.axis_size("tile")
    subsets = lax.axis_size("trace")
    myself = lax.axis_index("tile")
    _, block_count, block_rows, samples = traces.shape
    slots, taus = time_weights.shape[2:4]
    columns = amplitudes.shape[-1]
    half_taps = (taps.shape[1] - 1) // 2
    listing = lax.dynamic_index_in_dim(aperture[0], myself, 0, keepdims=False)
    fill = lax.dynamic_index_in_dim(counts[0], myself, 0, keepdims=False)
    order = jnp.arange(slots, dtype=jnp.int32)
    blocks = jnp.arange(tiles * block_count, dtype=jnp.int32)
    match = (listing[None, :] == blocks[:, None]) & (order < fill)[None, :]
    inv = jnp.sum(jnp.where(match, order[None, :], 0), axis=1, dtype=jnp.int32)
    alive = jnp.sum(match.astype(jnp.float32), axis=1)
    flipped = taps[:, ::-1].astype(jnp.float32)
    band = jnp.concatenate(
        [
            flipped[:, half_taps:],
            jnp.zeros((2, samples - taps.shape[1]), jnp.float32),
            flipped[:, :half_taps],
        ],
        axis=1,
    )
    chunk_rows = block_count * block_rows // halves
    share = taus // subsets
    rows_z = tiles // 2
    smem = pl.BlockSpec(memory_space=pltpu.SMEM)
    vmem = pl.BlockSpec(memory_space=pltpu.VMEM)
    hbm = pl.BlockSpec(memory_space=pl.ANY)
    image = pl.pallas_call(
        functools.partial(migrate_kernel, rows_z, subsets, half_taps),
        out_shape=jax.ShapeDtypeStruct((share, columns), jnp.float32),
        in_specs=[smem, smem, vmem, hbm, hbm, hbm],
        out_specs=vmem,
        scratch_shapes=[
            pltpu.VMEM((tiles, halves, chunk_rows, samples), jnp.bfloat16),
            pltpu.VMEM((slots, taus, samples), jnp.bfloat16),
            pltpu.VMEM((slots, 2, block_rows, columns), jnp.bfloat16),
            pltpu.VMEM((2 * samples, samples), jnp.bfloat16),
            pltpu.VMEM((2 * samples, chunk_rows), jnp.bfloat16),
            pltpu.VMEM((taus, columns), jnp.float32),
            pltpu.VMEM((subsets - 1, share, columns), jnp.float32),
            pltpu.SemaphoreType.DMA((tiles, halves)),
            pltpu.SemaphoreType.DMA((2, rows_z, halves)),
            pltpu.SemaphoreType.DMA((rows_z, halves)),
            pltpu.SemaphoreType.DMA((3,)),
            pltpu.SemaphoreType.DMA((subsets - 1,)),
            pltpu.SemaphoreType.DMA((subsets - 1,)),
        ],
        compiler_params=pltpu.CompilerParams(
            collective_id=0, has_side_effects=True, vmem_limit_bytes=48 * 1024 * 1024
        ),
    )(
        inv,
        alive,
        band,
        traces.reshape(halves, chunk_rows, samples),
        time_weights[0, 0],
        amplitudes[0, 0],
    )
    return image[None]


def filter_matrix(taps, samples):
    width = taps.shape[1]
    center = (width - 1) // 2
    offset = jnp.arange(samples)[:, None] - jnp.arange(samples)[None, :] + center
    table = (offset[:, :, None] == jnp.arange(width)[None, None, :]).astype(jnp.bfloat16)
    return jnp.einsum("ct,nmt->cnm", taps, table, preferred_element_type=jnp.float32).astype(
        jnp.bfloat16
    )


def exchange_per_device(traces, taps, aperture, counts, time_weights, amplitudes):
    tiles = lax.axis_size("tile")
    myself = lax.axis_index("tile")
    block_count = traces.shape[1]
    samples = traces.shape[3]
    slots = aperture.shape[2]
    capacity = max(2, slots // tiles)
    listing = aperture[0]
    filled = counts[0]
    owners = listing // block_count
    within = listing - owners * block_count
    order = jnp.arange(slots)
    earlier = order[None, :] < order[:, None]
    rank = jnp.sum((owners[:, :, None] == owners[:, None, :]) & earlier[None], axis=2)
    alive_slots = order[None, :] < filled[:, None]
    mine = (owners == myself) & alive_slots
    rank_onehot = (
        (rank[:, :, None] == jnp.arange(capacity)[None, None, :]) & mine[:, :, None]
    ).astype(jnp.bfloat16)
    local_onehot = (within[:, :, None] == jnp.arange(block_count)[None, None, :]).astype(
        jnp.bfloat16
    )
    select = jnp.einsum(
        "ksc,ksl->kcl", rank_onehot, local_onehot, preferred_element_type=jnp.float32
    ).astype(jnp.bfloat16)
    operator = filter_matrix(taps, samples)
    own_owner = lax.dynamic_index_in_dim(owners, myself, 0, keepdims=False)
    own_rank = lax.dynamic_index_in_dim(rank, myself, 0, keepdims=False)
    own_fill = lax.dynamic_index_in_dim(filled, myself, 0, keepdims=False)
    source_slot = own_owner * capacity + own_rank
    arrived_rows = tiles * capacity

    def pick_rows(positions):
        return (positions[:, None] == jnp.arange(arrived_rows)[None, :]).astype(jnp.bfloat16)

    filtered = jnp.einsum(
        "cnm,kbm->kcbn", operator, traces[0], preferred_element_type=jnp.float32
    ).astype(jnp.bfloat16)
    outgoing = jnp.einsum(
        "kcl,lqbn->kcqbn", select, filtered, preferred_element_type=jnp.float32
    ).astype(jnp.bfloat16)
    arrived = lax.all_to_all(outgoing, "tile", split_axis=0, concat_axis=0, tiled=True)
    arrived = arrived.reshape((arrived_rows,) + arrived.shape[2:])

    def fetch(positions):
        return jnp.einsum(
            "gq,qcbn->gcbn", pick_rows(positions), arrived, preferred_element_type=jnp.float32
        ).astype(jnp.bfloat16)

    weights = time_weights[0, 0]
    spread = amplitudes[0, 0]

    def add_group(index, total):
        start = index * group_slots
        positions = lax.dynamic_slice_in_dim(source_slot, start, group_slots, 0)
        blocks = fetch(positions)
        part_weights = lax.dynamic_slice_in_dim(weights, start, group_slots, 0)
        part_spread = lax.dynamic_slice_in_dim(spread, start, group_slots, 0)
        alive = (start + jnp.arange(group_slots) < own_fill).astype(jnp.float32)
        interp = jnp.einsum(
            "gtn,gcbn->gcbt", part_weights, blocks, preferred_element_type=jnp.float32
        )
        interp = (interp * alive[:, None, None, None]).astype(jnp.bfloat16)
        return total + jnp.einsum(
            "gcbt,gcbp->tp", interp, part_spread, preferred_element_type=jnp.float32
        )

    rounds = (own_fill + group_slots - 1) // group_slots
    partial_value = lax.fori_loop(
        0, rounds, add_group, jnp.zeros((weights.shape[1], spread.shape[-1]), jnp.float32)
    )
    image = lax.psum_scatter(partial_value, "trace", scatter_dimension=0, tiled=True)
    return image[None]


def per_device(traces, taps, aperture, counts, time_weights, amplitudes):
    tiles = lax.axis_size("tile")
    every_block = traces.shape[1] * tiles
    form = gather_per_device if every_block == aperture.shape[2] else exchange_per_device
    return form(traces, taps, aperture, counts, time_weights, amplitudes)


def solution(mesh):
    placed = (
        P("trace", "tile", None, None),
        P(),
        P("trace", None, None),
        P("trace", None),
        P("trace", "tile", None, None, None),
        P("trace", "tile", None, None, None, None),
    )
    return jax.shard_map(
        per_device, mesh=mesh, in_specs=placed, out_specs=P("tile", "trace", None), check_vma=False
    )
```

```python
import functools

import jax
import jax.numpy as jnp
from jax import lax
from jax.experimental import pallas as pl
from jax.experimental.pallas import tpu as pltpu
from jax.sharding import PartitionSpec as P

group_slots = 8
lane_group = 4
halves = 2
relay_from = 1
MESH = pl.DeviceIdType.MESH


def migrate_kernel(
    rows_z,
    subsets,
    counts_hbm,
    aperture_hbm,
    taps_hbm,
    traces_ref,
    weights_ref,
    spread_ref,
    out_ref,
    gathered,
    weights,
    spread,
    operator,
    filtered,
    total,
    parts,
    counts_ref,
    aperture_ref,
    taps_ref,
    band,
    lookup,
    slot_of,
    recv_sem,
    send_z_sem,
    send_x_sem,
    relay_sem,
    load_sem,
    part_send_sem,
    part_recv_sem,
):
    tile = lax.axis_index("tile")
    subset = lax.axis_index("trace")
    z = tile // 2
    x = tile % 2
    other = 1 - x
    samples = operator.shape[1]
    chunk_rows = gathered.shape[2]
    block_rows = spread.shape[2]
    chunk_blocks = chunk_rows // block_rows
    block_count = chunk_blocks * halves
    group_lanes = lane_group * block_rows

    load_small = [
        pltpu.make_async_copy(src, dst, load_sem.at[4 + at])
        for at, (src, dst) in enumerate(
            ((counts_hbm, counts_ref), (aperture_hbm, aperture_ref), (taps_hbm, taps_ref))
        )
    ]
    load_own = pltpu.make_async_copy(traces_ref, gathered.at[tile], load_sem.at[0])
    load_weights = pltpu.make_async_copy(weights_ref, weights, load_sem.at[1])
    load_spread = pltpu.make_async_copy(spread_ref, spread, load_sem.at[2])

    barrier = pltpu.get_barrier_semaphore()

    @pl.when(z > 0)
    def _():
        pl.semaphore_signal(barrier, inc=1, device_id=(tile - 2, subset), device_id_type=MESH)

    @pl.when(z < rows_z - 1)
    def _():
        pl.semaphore_signal(barrier, inc=1, device_id=(tile + 2, subset), device_id_type=MESH)

    pl.semaphore_signal(barrier, inc=1, device_id=(z * 2 + other, subset), device_id_type=MESH)
    for step in range(1, subsets):
        pl.semaphore_signal(
            barrier, inc=1, device_id=(tile, (subset + step) % subsets), device_id_type=MESH
        )
    for load in load_small:
        load.start()
    load_own.start()
    inner = jnp.where((z > 0) & (z < rows_z - 1), 1, 0)
    pl.semaphore_wait(barrier, subsets + 1 + inner)

    def source(origin_z, half, own):
        if own:
            return traces_ref.at[half]
        return gathered.at[origin_z * 2 + x, half]

    def send_z(origin_z, half, up, own=False):
        return pltpu.make_async_remote_copy(
            src_ref=source(origin_z, half, own),
            dst_ref=gathered.at[origin_z * 2 + x, half],
            send_sem=send_z_sem.at[up, origin_z, half],
            recv_sem=recv_sem.at[origin_z * 2 + x, half],
            device_id=(tile + 4 * up - 2, subset),
            device_id_type=MESH,
        )

    def send_x(origin_z, half, own=False):
        return pltpu.make_async_remote_copy(
            src_ref=source(origin_z, half, own),
            dst_ref=gathered.at[origin_z * 2 + x, half],
            send_sem=send_x_sem.at[origin_z, half],
            recv_sem=recv_sem.at[origin_z * 2 + x, half],
            device_id=(z * 2 + other, subset),
            device_id_type=MESH,
        )

    pair_z = z + 1 - 2 * (z % 2)

    def relay(half):
        return pltpu.make_async_remote_copy(
            src_ref=gathered.at[z * 2 + other, half],
            dst_ref=gathered.at[z * 2 + other, half],
            send_sem=relay_sem.at[half],
            recv_sem=recv_sem.at[z * 2 + other, half],
            device_id=(pair_z * 2 + x, subset),
            device_id_type=MESH,
        )

    def wait_arrival(origin, half):
        pltpu.make_async_remote_copy(
            src_ref=gathered.at[origin, half],
            dst_ref=gathered.at[origin, half],
            send_sem=send_x_sem.at[0, 0],
            recv_sem=recv_sem.at[origin, half],
            device_id=(z * 2 + other, subset),
            device_id_type=MESH,
        ).wait_recv()

    for half in range(halves):

        @pl.when(z < rows_z - 1)
        def _():
            send_z(z, half, 1, True).start()

        @pl.when(z > 0)
        def _():
            send_z(z, half, 0, True).start()

        send_x(z, half, True).start()

    load_weights.start()
    load_spread.start()
    for load in load_small:
        load.wait()
    slots = weights.shape[0]
    listing = aperture_ref[0, pl.ds(tile, 1), :]
    slot = lax.broadcasted_iota(jnp.int32, (slots, slots), 0)
    block = lax.broadcasted_iota(jnp.int32, (slots, slots), 1)
    named = jnp.broadcast_to(listing, (slots, slots)).T
    match = (named == block) & (slot < counts_ref[0, tile])
    lookup[...] = jnp.broadcast_to(
        jnp.sum(jnp.where(match, slot + 1, 0), axis=0, keepdims=True) - 1, lookup.shape
    )
    publish = pltpu.make_async_copy(lookup, slot_of, load_sem.at[3])
    publish.start()

    half_taps = (taps_ref.shape[1] - 1) // 2
    band[...] = jnp.zeros_like(band)
    band[0:2, 0 : taps_ref.shape[1]] = taps_ref[...].astype(jnp.float32)
    row = lax.broadcasted_iota(jnp.int32, (samples, samples), 0)
    gap = lax.broadcasted_iota(jnp.int32, (samples, samples), 1) - row
    inside = (gap <= half_taps) & (gap >= -half_taps)
    for channel in range(2):
        centred = pltpu.roll(band[...], samples - half_taps, 1)[channel : channel + 1, :]
        shifted = jnp.broadcast_to(centred, (samples, samples))
        shift = 1
        while shift < samples:
            shifted = jnp.where((row // shift) % 2 == 1, pltpu.roll(shifted, shift, 1), shifted)
            shift *= 2
        operator[channel * samples : (channel + 1) * samples, :] = (
            jnp.where(inside, shifted, 0.0).T
        ).astype(operator.dtype)
    total[...] = jnp.zeros_like(total)

    lanes = lax.broadcasted_iota(jnp.int32, (1, 2 * group_lanes), 1)
    member = (lanes // block_rows) % lane_group

    def compute(origin, half):
        filtered[...] = lax.dot_general(
            operator[...],
            gathered[origin, half],
            (((1,), (1,)), ((), ())),
            preferred_element_type=jnp.float32,
        ).astype(filtered.dtype)
        taus = weights.shape[1]
        for group in range(chunk_blocks // lane_group):
            first = group * group_lanes
            blocks = jnp.concatenate(
                [
                    filtered[0:samples, first : first + group_lanes],
                    filtered[samples : 2 * samples, first : first + group_lanes],
                ],
                axis=1,
            )
            base = origin * block_count + half * chunk_blocks + group * lane_group
            found = [slot_of[0, base + index] for index in range(lane_group)]
            picks = [jnp.maximum(value, 0) for value in found]
            gains = [jnp.where(value >= 0, 1.0, 0.0) for value in found]
            stacked = jnp.concatenate([weights[pick] for pick in picks], axis=0)
            product = jnp.dot(stacked, blocks, preferred_element_type=jnp.float32)
            interp = product[0:taus]
            alive = jnp.full((1, 2 * group_lanes), gains[0], jnp.float32)
            for index in range(1, lane_group):
                here = member == index
                interp = jnp.where(here, product[index * taus : (index + 1) * taus], interp)
                alive = jnp.where(here, gains[index], alive)
            interp = (interp * alive).astype(jnp.bfloat16)
            columns = jnp.concatenate(
                [spread[pick, channel] for channel in range(2) for pick in picks], axis=0
            )
            total[...] += jnp.dot(interp, columns, preferred_element_type=jnp.float32)

    load_own.wait()
    load_weights.wait()
    load_spread.wait()
    publish.wait()

    def own_chunk(half, carry):
        compute(tile, half)
        return carry

    lax.fori_loop(0, halves, own_chunk, 0)

    for distance in range(1, rows_z + 1):
        for half in range(halves):
            for up in (1, 0):
                origin_z = z - distance if up else z + distance

                @pl.when((origin_z >= 0) & (origin_z < rows_z))
                def _():
                    wait_arrival(origin_z * 2 + x, half)

                    @pl.when((z > 0) & (z < rows_z - 1))
                    def _():
                        send_z(origin_z, half, up).start()

                    if half < relay_from:
                        send_x(origin_z, half).start()
                    else:

                        @pl.when(origin_z != pair_z)
                        def _():
                            send_x(origin_z, half).start()

        if distance == 2:
            for half in range(relay_from, halves):
                relay(half).start()

        def column_chunk(event, carry):
            half = event // 2
            up = event % 2
            near = z - distance * (2 * up - 1)
            far = z - (distance - 1) * (2 * up - 1)

            @pl.when((near >= 0) & (near < rows_z))
            def _():
                compute(near * 2 + x, half)

            if distance > 1:
                wanted = (far >= 0) & (far < rows_z)
            else:
                wanted = up == 1

            @pl.when(wanted)
            def _():
                wait_arrival(far * 2 + other, half)
                compute(far * 2 + other, half)

            return carry

        lax.fori_loop(0, 2 * halves, column_chunk, 0)

    share = out_ref.shape[0]
    sends = []
    for step in range(1, subsets):
        peer = (subset + step) % subsets
        copy = pltpu.make_async_remote_copy(
            src_ref=total.at[pl.ds(pl.multiple_of(peer * share, share), share)],
            dst_ref=parts.at[step - 1],
            send_sem=part_send_sem.at[step - 1],
            recv_sem=part_recv_sem.at[step - 1],
            device_id=(tile, peer),
            device_id_type=MESH,
        )
        copy.start()
        sends.append(copy)
    result = total[pl.ds(pl.multiple_of(subset * share, share), share), :]
    for step in range(1, subsets):
        sends[step - 1].wait_recv()
        result = result + parts[step - 1]
    out_ref[...] = result
    for copy in sends:
        copy.wait_send()

    for half in range(halves):

        @pl.when(z < rows_z - 1)
        def _():
            send_z(z, half, 1, True).wait_send()

        @pl.when(z > 0)
        def _():
            send_z(z, half, 0, True).wait_send()

        send_x(z, half, True).wait_send()
        for distance in range(1, rows_z):
            for up in (1, 0):
                origin_z = z - distance if up else z + distance

                @pl.when((origin_z >= 0) & (origin_z < rows_z))
                def _():
                    @pl.when((z > 0) & (z < rows_z - 1))
                    def _():
                        send_z(origin_z, half, up).wait_send()

                    if half < relay_from:
                        send_x(origin_z, half).wait_send()
                    else:

                        @pl.when(origin_z != pair_z)
                        def _():
                            send_x(origin_z, half).wait_send()

    for half in range(relay_from, halves):
        relay(half).wait_send()


def gather_per_device(traces, taps, aperture, counts, time_weights, amplitudes):
    tiles = lax.axis_size("tile")
    subsets = lax.axis_size("trace")
    _, block_count, block_rows, samples = traces.shape
    slots, taus = time_weights.shape[2:4]
    columns = amplitudes.shape[-1]
    chunk_rows = block_count * block_rows // halves
    share = taus // subsets
    rows_z = tiles // 2
    vmem = pl.BlockSpec(memory_space=pltpu.VMEM)
    hbm = pl.BlockSpec(memory_space=pl.ANY)
    image = pl.pallas_call(
        functools.partial(migrate_kernel, rows_z, subsets),
        out_shape=jax.ShapeDtypeStruct((share, columns), jnp.float32),
        in_specs=[hbm] * 6,
        out_specs=vmem,
        scratch_shapes=[
            pltpu.VMEM((tiles, halves, chunk_rows, samples), jnp.bfloat16),
            pltpu.VMEM((slots, taus, samples), jnp.bfloat16),
            pltpu.VMEM((slots, 2, block_rows, columns), jnp.bfloat16),
            pltpu.VMEM((2 * samples, samples), jnp.bfloat16),
            pltpu.VMEM((2 * samples, chunk_rows), jnp.bfloat16),
            pltpu.VMEM((taus, columns), jnp.float32),
            pltpu.VMEM((subsets - 1, share, columns), jnp.float32),
            pltpu.SMEM(counts.shape, jnp.int32),
            pltpu.VMEM(aperture.shape, jnp.int32),
            pltpu.VMEM(taps.shape, taps.dtype),
            pltpu.VMEM((8, samples), jnp.float32),
            pltpu.VMEM((8, slots), jnp.int32),
            pltpu.SMEM((8, slots), jnp.int32),
            pltpu.SemaphoreType.DMA((tiles, halves)),
            pltpu.SemaphoreType.DMA((2, rows_z, halves)),
            pltpu.SemaphoreType.DMA((rows_z, halves)),
            pltpu.SemaphoreType.DMA((halves,)),
            pltpu.SemaphoreType.DMA((7,)),
            pltpu.SemaphoreType.DMA((subsets - 1,)),
            pltpu.SemaphoreType.DMA((subsets - 1,)),
        ],
        compiler_params=pltpu.CompilerParams(
            collective_id=0, has_side_effects=True, vmem_limit_bytes=62 * 1024 * 1024
        ),
    )(
        counts,
        aperture,
        taps,
        traces.reshape(halves, chunk_rows, samples),
        time_weights[0, 0],
        amplitudes[0, 0],
    )
    return image[None]


def filter_matrix(taps, samples):
    width = taps.shape[1]
    center = (width - 1) // 2
    offset = jnp.arange(samples)[:, None] - jnp.arange(samples)[None, :] + center
    table = (offset[:, :, None] == jnp.arange(width)[None, None, :]).astype(jnp.bfloat16)
    return jnp.einsum("ct,nmt->cnm", taps, table, preferred_element_type=jnp.float32).astype(
        jnp.bfloat16
    )


def exchange_per_device(traces, taps, aperture, counts, time_weights, amplitudes):
    tiles = lax.axis_size("tile")
    myself = lax.axis_index("tile")
    block_count = traces.shape[1]
    samples = traces.shape[3]
    slots = aperture.shape[2]
    capacity = max(2, slots // tiles)
    listing = aperture[0]
    filled = counts[0]
    owners = listing // block_count
    within = listing - owners * block_count
    order = jnp.arange(slots)
    earlier = order[None, :] < order[:, None]
    rank = jnp.sum((owners[:, :, None] == owners[:, None, :]) & earlier[None], axis=2)
    alive_slots = order[None, :] < filled[:, None]
    mine = (owners == myself) & alive_slots
    rank_onehot = (
        (rank[:, :, None] == jnp.arange(capacity)[None, None, :]) & mine[:, :, None]
    ).astype(jnp.bfloat16)
    local_onehot = (within[:, :, None] == jnp.arange(block_count)[None, None, :]).astype(
        jnp.bfloat16
    )
    select = jnp.einsum(
        "ksc,ksl->kcl", rank_onehot, local_onehot, preferred_element_type=jnp.float32
    ).astype(jnp.bfloat16)
    operator = filter_matrix(taps, samples)
    own_owner = lax.dynamic_index_in_dim(owners, myself, 0, keepdims=False)
    own_rank = lax.dynamic_index_in_dim(rank, myself, 0, keepdims=False)
    own_fill = lax.dynamic_index_in_dim(filled, myself, 0, keepdims=False)
    source_slot = own_owner * capacity + own_rank
    arrived_rows = tiles * capacity

    def pick_rows(positions):
        return (positions[:, None] == jnp.arange(arrived_rows)[None, :]).astype(jnp.bfloat16)

    filtered = jnp.einsum(
        "cnm,kbm->kcbn", operator, traces[0], preferred_element_type=jnp.float32
    ).astype(jnp.bfloat16)
    outgoing = jnp.einsum(
        "kcl,lqbn->kcqbn", select, filtered, preferred_element_type=jnp.float32
    ).astype(jnp.bfloat16)
    arrived = lax.all_to_all(outgoing, "tile", split_axis=0, concat_axis=0, tiled=True)
    arrived = arrived.reshape((arrived_rows,) + arrived.shape[2:])

    def fetch(positions):
        return jnp.einsum(
            "gq,qcbn->gcbn", pick_rows(positions), arrived, preferred_element_type=jnp.float32
        ).astype(jnp.bfloat16)

    weights = time_weights[0, 0]
    spread = amplitudes[0, 0]

    def add_group(index, total):
        start = index * group_slots
        positions = lax.dynamic_slice_in_dim(source_slot, start, group_slots, 0)
        blocks = fetch(positions)
        part_weights = lax.dynamic_slice_in_dim(weights, start, group_slots, 0)
        part_spread = lax.dynamic_slice_in_dim(spread, start, group_slots, 0)
        alive = (start + jnp.arange(group_slots) < own_fill).astype(jnp.float32)
        interp = jnp.einsum(
            "gtn,gcbn->gcbt", part_weights, blocks, preferred_element_type=jnp.float32
        )
        interp = (interp * alive[:, None, None, None]).astype(jnp.bfloat16)
        return total + jnp.einsum(
            "gcbt,gcbp->tp", interp, part_spread, preferred_element_type=jnp.float32
        )

    rounds = (own_fill + group_slots - 1) // group_slots
    partial_value = lax.fori_loop(
        0, rounds, add_group, jnp.zeros((weights.shape[1], spread.shape[-1]), jnp.float32)
    )
    image = lax.psum_scatter(partial_value, "trace", scatter_dimension=0, tiled=True)
    return image[None]


def per_device(traces, taps, aperture, counts, time_weights, amplitudes):
    tiles = lax.axis_size("tile")
    every_block = traces.shape[1] * tiles
    gathers = every_block == aperture.shape[2] and tiles % 4 == 0
    form = gather_per_device if gathers else exchange_per_device
    return form(traces, taps, aperture, counts, time_weights, amplitudes)


def solution(mesh):
    placed = (
        P("trace", "tile", None, None),
        P(),
        P("trace", None, None),
        P("trace", None),
        P("trace", "tile", None, None, None),
        P("trace", "tile", None, None, None, None),
    )
    return jax.shard_map(
        per_device, mesh=mesh, in_specs=placed, out_specs=P("tile", "trace", None), check_vma=False
    )
```

```python
import functools

import jax
import jax.numpy as jnp
from jax import lax
from jax.experimental import pallas as pl
from jax.experimental.pallas import tpu as pltpu
from jax.sharding import PartitionSpec as P

group_slots = 8
lane_group = 4
halves = 2
relay_from = 2
MESH = pl.DeviceIdType.MESH


def migrate_kernel(
    rows_z,
    subsets,
    counts_hbm,
    aperture_hbm,
    taps_hbm,
    traces_ref,
    weights_ref,
    spread_ref,
    out_ref,
    gathered,
    weights,
    spread,
    operator,
    filtered,
    total,
    parts,
    counts_ref,
    aperture_ref,
    taps_ref,
    band,
    lookup,
    slot_of,
    recv_sem,
    send_z_sem,
    send_x_sem,
    relay_sem,
    load_sem,
    part_send_sem,
    part_recv_sem,
):
    tile = lax.axis_index("tile")
    subset = lax.axis_index("trace")
    z = tile // 2
    x = tile % 2
    other = 1 - x
    samples = operator.shape[1]
    chunk_rows = gathered.shape[2]
    block_rows = spread.shape[2]
    chunk_blocks = chunk_rows // block_rows
    block_count = chunk_blocks * halves
    group_lanes = lane_group * block_rows

    load_small = [
        pltpu.make_async_copy(src, dst, load_sem.at[4 + at])
        for at, (src, dst) in enumerate(
            ((counts_hbm, counts_ref), (aperture_hbm, aperture_ref), (taps_hbm, taps_ref))
        )
    ]
    load_own = pltpu.make_async_copy(traces_ref, gathered.at[tile], load_sem.at[0])
    load_weights = pltpu.make_async_copy(weights_ref, weights, load_sem.at[1])
    load_spread = pltpu.make_async_copy(spread_ref, spread, load_sem.at[2])

    barrier = pltpu.get_barrier_semaphore()

    @pl.when(z > 0)
    def _():
        pl.semaphore_signal(barrier, inc=1, device_id=(tile - 2, subset), device_id_type=MESH)

    @pl.when(z < rows_z - 1)
    def _():
        pl.semaphore_signal(barrier, inc=1, device_id=(tile + 2, subset), device_id_type=MESH)

    pl.semaphore_signal(barrier, inc=1, device_id=(z * 2 + other, subset), device_id_type=MESH)
    for step in range(1, subsets):
        pl.semaphore_signal(
            barrier, inc=1, device_id=(tile, (subset + step) % subsets), device_id_type=MESH
        )
    for load in load_small:
        load.start()
    load_own.start()
    inner = jnp.where((z > 0) & (z < rows_z - 1), 1, 0)
    pl.semaphore_wait(barrier, subsets + 1 + inner)

    def source(origin_z, half, own):
        if own:
            return traces_ref.at[half]
        return gathered.at[origin_z * 2 + x, half]

    def send_z(origin_z, half, up, own=False):
        return pltpu.make_async_remote_copy(
            src_ref=source(origin_z, half, own),
            dst_ref=gathered.at[origin_z * 2 + x, half],
            send_sem=send_z_sem.at[up, origin_z, half],
            recv_sem=recv_sem.at[origin_z * 2 + x, half],
            device_id=(tile + 4 * up - 2, subset),
            device_id_type=MESH,
        )

    def send_x(origin_z, half, own=False):
        return pltpu.make_async_remote_copy(
            src_ref=source(origin_z, half, own),
            dst_ref=gathered.at[origin_z * 2 + x, half],
            send_sem=send_x_sem.at[origin_z, half],
            recv_sem=recv_sem.at[origin_z * 2 + x, half],
            device_id=(z * 2 + other, subset),
            device_id_type=MESH,
        )

    pair_z = z + 1 - 2 * (z % 2)

    def relay(half):
        return pltpu.make_async_remote_copy(
            src_ref=gathered.at[z * 2 + other, half],
            dst_ref=gathered.at[z * 2 + other, half],
            send_sem=relay_sem.at[half],
            recv_sem=recv_sem.at[z * 2 + other, half],
            device_id=(pair_z * 2 + x, subset),
            device_id_type=MESH,
        )

    def wait_arrival(origin, half):
        pltpu.make_async_remote_copy(
            src_ref=gathered.at[origin, half],
            dst_ref=gathered.at[origin, half],
            send_sem=send_x_sem.at[0, 0],
            recv_sem=recv_sem.at[origin, half],
            device_id=(z * 2 + other, subset),
            device_id_type=MESH,
        ).wait_recv()

    for half in range(halves):

        @pl.when(z < rows_z - 1)
        def _():
            send_z(z, half, 1, True).start()

        @pl.when(z > 0)
        def _():
            send_z(z, half, 0, True).start()

        send_x(z, half, True).start()

    load_weights.start()
    load_spread.start()
    for load in load_small:
        load.wait()
    slots = weights.shape[0]
    listing = aperture_ref[0, pl.ds(tile, 1), :]
    slot = lax.broadcasted_iota(jnp.int32, (slots, slots), 0)
    block = lax.broadcasted_iota(jnp.int32, (slots, slots), 1)
    named = jnp.broadcast_to(listing, (slots, slots)).T
    match = (named == block) & (slot < counts_ref[0, tile])
    lookup[...] = jnp.broadcast_to(
        jnp.sum(jnp.where(match, slot + 1, 0), axis=0, keepdims=True) - 1, lookup.shape
    )
    publish = pltpu.make_async_copy(lookup, slot_of, load_sem.at[3])
    publish.start()

    half_taps = (taps_ref.shape[1] - 1) // 2
    band[...] = jnp.zeros_like(band)
    band[0:2, 0 : taps_ref.shape[1]] = taps_ref[...].astype(jnp.float32)
    row = lax.broadcasted_iota(jnp.int32, (samples, samples), 0)
    gap = lax.broadcasted_iota(jnp.int32, (samples, samples), 1) - row
    inside = (gap <= half_taps) & (gap >= -half_taps)
    for channel in range(2):
        centred = pltpu.roll(band[...], samples - half_taps, 1)[channel : channel + 1, :]
        shifted = jnp.broadcast_to(centred, (samples, samples))
        shift = 1
        while shift < samples:
            shifted = jnp.where((row // shift) % 2 == 1, pltpu.roll(shifted, shift, 1), shifted)
            shift *= 2
        operator[channel * samples : (channel + 1) * samples, :] = (
            jnp.where(inside, shifted, 0.0).T
        ).astype(operator.dtype)
    total[...] = jnp.zeros_like(total)

    lanes = lax.broadcasted_iota(jnp.int32, (1, 2 * group_lanes), 1)
    member = (lanes // block_rows) % lane_group

    def compute(origin, half):
        filtered[...] = lax.dot_general(
            operator[...],
            gathered[origin, half],
            (((1,), (1,)), ((), ())),
            preferred_element_type=jnp.float32,
        ).astype(filtered.dtype)
        taus = weights.shape[1]
        for group in range(chunk_blocks // lane_group):
            first = group * group_lanes
            blocks = jnp.concatenate(
                [
                    filtered[0:samples, first : first + group_lanes],
                    filtered[samples : 2 * samples, first : first + group_lanes],
                ],
                axis=1,
            )
            base = origin * block_count + half * chunk_blocks + group * lane_group
            found = [slot_of[0, base + index] for index in range(lane_group)]
            picks = [jnp.maximum(value, 0) for value in found]
            gains = [jnp.where(value >= 0, 1.0, 0.0) for value in found]
            stacked = jnp.concatenate([weights[pick] for pick in picks], axis=0)
            product = jnp.dot(stacked, blocks, preferred_element_type=jnp.float32)
            interp = product[0:taus]
            alive = jnp.full((1, 2 * group_lanes), gains[0], jnp.float32)
            for index in range(1, lane_group):
                here = member == index
                interp = jnp.where(here, product[index * taus : (index + 1) * taus], interp)
                alive = jnp.where(here, gains[index], alive)
            interp = (interp * alive).astype(jnp.bfloat16)
            columns = jnp.concatenate(
                [spread[pick, channel] for channel in range(2) for pick in picks], axis=0
            )
            total[...] += jnp.dot(interp, columns, preferred_element_type=jnp.float32)

    load_own.wait()
    load_weights.wait()
    load_spread.wait()
    publish.wait()

    def own_chunk(half, carry):
        compute(tile, half)
        return carry

    lax.fori_loop(0, halves, own_chunk, 0)

    for distance in range(1, rows_z + 1):
        for half in range(halves):
            for up in (1, 0):
                origin_z = z - distance if up else z + distance

                @pl.when((origin_z >= 0) & (origin_z < rows_z))
                def _():
                    wait_arrival(origin_z * 2 + x, half)

                    @pl.when((z > 0) & (z < rows_z - 1))
                    def _():
                        send_z(origin_z, half, up).start()

                    if half < relay_from:
                        send_x(origin_z, half).start()
                    else:

                        @pl.when(origin_z != pair_z)
                        def _():
                            send_x(origin_z, half).start()

            def column_chunk(event, carry):
                half = event // 2
                up = event % 2
                near = z - distance * (2 * up - 1)
                far = z - (distance - 1) * (2 * up - 1)

                @pl.when((near >= 0) & (near < rows_z))
                def _():
                    compute(near * 2 + x, half)

                wanted = (far >= 0) & (far < rows_z)
                if distance == 1:
                    wanted = up == 1
                if distance == 2:
                    wanted = wanted & ((half < relay_from) | (far != pair_z))

                @pl.when(wanted)
                def _():
                    wait_arrival(far * 2 + other, half)
                    compute(far * 2 + other, half)

                return carry

            lax.fori_loop(2 * half, 2 * half + 2, column_chunk, 0)

    def relayed_chunk(half, carry):
        wait_arrival(pair_z * 2 + other, half)
        compute(pair_z * 2 + other, half)
        return carry

    lax.fori_loop(relay_from, halves, relayed_chunk, 0)

    share = out_ref.shape[0]
    sends = []
    for step in range(1, subsets):
        peer = (subset + step) % subsets
        copy = pltpu.make_async_remote_copy(
            src_ref=total.at[pl.ds(pl.multiple_of(peer * share, share), share)],
            dst_ref=parts.at[step - 1],
            send_sem=part_send_sem.at[step - 1],
            recv_sem=part_recv_sem.at[step - 1],
            device_id=(tile, peer),
            device_id_type=MESH,
        )
        copy.start()
        sends.append(copy)
    result = total[pl.ds(pl.multiple_of(subset * share, share), share), :]
    for step in range(1, subsets):
        sends[step - 1].wait_recv()
        result = result + parts[step - 1]
    out_ref[...] = result
    for copy in sends:
        copy.wait_send()

    for half in range(halves):

        @pl.when(z < rows_z - 1)
        def _():
            send_z(z, half, 1, True).wait_send()

        @pl.when(z > 0)
        def _():
            send_z(z, half, 0, True).wait_send()

        send_x(z, half, True).wait_send()
        for distance in range(1, rows_z):
            for up in (1, 0):
                origin_z = z - distance if up else z + distance

                @pl.when((origin_z >= 0) & (origin_z < rows_z))
                def _():
                    @pl.when((z > 0) & (z < rows_z - 1))
                    def _():
                        send_z(origin_z, half, up).wait_send()

                    if half < relay_from:
                        send_x(origin_z, half).wait_send()
                    else:

                        @pl.when(origin_z != pair_z)
                        def _():
                            send_x(origin_z, half).wait_send()

    for half in range(relay_from, halves):
        relay(half).wait_send()


def keep(array):
    return pltpu.with_memory_space_constraint(array, pltpu.HBM)


def gather_per_device(traces, taps, aperture, counts, time_weights, amplitudes):
    tiles = lax.axis_size("tile")
    subsets = lax.axis_size("trace")
    _, block_count, block_rows, samples = traces.shape
    slots, taus = time_weights.shape[2:4]
    columns = amplitudes.shape[-1]
    chunk_rows = block_count * block_rows // halves
    share = taus // subsets
    rows_z = tiles // 2
    vmem = pl.BlockSpec(memory_space=pltpu.VMEM)
    hbm = pl.BlockSpec(memory_space=pl.ANY)
    image = pl.pallas_call(
        functools.partial(migrate_kernel, rows_z, subsets),
        out_shape=jax.ShapeDtypeStruct((share, columns), jnp.float32),
        in_specs=[hbm] * 6,
        out_specs=vmem,
        scratch_shapes=[
            pltpu.VMEM((tiles, halves, chunk_rows, samples), jnp.bfloat16),
            pltpu.VMEM((slots, taus, samples), jnp.bfloat16),
            pltpu.VMEM((slots, 2, block_rows, columns), jnp.bfloat16),
            pltpu.VMEM((2 * samples, samples), jnp.bfloat16),
            pltpu.VMEM((2 * samples, chunk_rows), jnp.bfloat16),
            pltpu.VMEM((taus, columns), jnp.float32),
            pltpu.VMEM((subsets - 1, share, columns), jnp.float32),
            pltpu.SMEM(counts.shape, jnp.int32),
            pltpu.VMEM(aperture.shape, jnp.int32),
            pltpu.VMEM(taps.shape, taps.dtype),
            pltpu.VMEM((8, samples), jnp.float32),
            pltpu.VMEM((8, slots), jnp.int32),
            pltpu.SMEM((8, slots), jnp.int32),
            pltpu.SemaphoreType.DMA((tiles, halves)),
            pltpu.SemaphoreType.DMA((2, rows_z, halves)),
            pltpu.SemaphoreType.DMA((rows_z, halves)),
            pltpu.SemaphoreType.DMA((halves,)),
            pltpu.SemaphoreType.DMA((7,)),
            pltpu.SemaphoreType.DMA((subsets - 1,)),
            pltpu.SemaphoreType.DMA((subsets - 1,)),
        ],
        compiler_params=pltpu.CompilerParams(
            collective_id=0, has_side_effects=True, vmem_limit_bytes=48 * 1024 * 1024
        ),
    )(
        keep(counts),
        keep(aperture),
        keep(taps),
        keep(traces.reshape(halves, chunk_rows, samples)),
        keep(time_weights[0, 0]),
        keep(amplitudes[0, 0]),
    )
    return image[None]


def filter_matrix(taps, samples):
    width = taps.shape[1]
    center = (width - 1) // 2
    offset = jnp.arange(samples)[:, None] - jnp.arange(samples)[None, :] + center
    table = (offset[:, :, None] == jnp.arange(width)[None, None, :]).astype(jnp.bfloat16)
    return jnp.einsum("ct,nmt->cnm", taps, table, preferred_element_type=jnp.float32).astype(
        jnp.bfloat16
    )


def exchange_per_device(traces, taps, aperture, counts, time_weights, amplitudes):
    tiles = lax.axis_size("tile")
    myself = lax.axis_index("tile")
    block_count = traces.shape[1]
    samples = traces.shape[3]
    slots = aperture.shape[2]
    capacity = max(2, slots // tiles)
    listing = aperture[0]
    filled = counts[0]
    owners = listing // block_count
    within = listing - owners * block_count
    order = jnp.arange(slots)
    earlier = order[None, :] < order[:, None]
    rank = jnp.sum((owners[:, :, None] == owners[:, None, :]) & earlier[None], axis=2)
    alive_slots = order[None, :] < filled[:, None]
    mine = (owners == myself) & alive_slots
    rank_onehot = (
        (rank[:, :, None] == jnp.arange(capacity)[None, None, :]) & mine[:, :, None]
    ).astype(jnp.bfloat16)
    local_onehot = (within[:, :, None] == jnp.arange(block_count)[None, None, :]).astype(
        jnp.bfloat16
    )
    select = jnp.einsum(
        "ksc,ksl->kcl", rank_onehot, local_onehot, preferred_element_type=jnp.float32
    ).astype(jnp.bfloat16)
    operator = filter_matrix(taps, samples)
    own_owner = lax.dynamic_index_in_dim(owners, myself, 0, keepdims=False)
    own_rank = lax.dynamic_index_in_dim(rank, myself, 0, keepdims=False)
    own_fill = lax.dynamic_index_in_dim(filled, myself, 0, keepdims=False)
    source_slot = own_owner * capacity + own_rank
    arrived_rows = tiles * capacity

    def pick_rows(positions):
        return (positions[:, None] == jnp.arange(arrived_rows)[None, :]).astype(jnp.bfloat16)

    filtered = jnp.einsum(
        "cnm,kbm->kcbn", operator, traces[0], preferred_element_type=jnp.float32
    ).astype(jnp.bfloat16)
    outgoing = jnp.einsum(
        "kcl,lqbn->kcqbn", select, filtered, preferred_element_type=jnp.float32
    ).astype(jnp.bfloat16)
    arrived = lax.all_to_all(outgoing, "tile", split_axis=0, concat_axis=0, tiled=True)
    arrived = arrived.reshape((arrived_rows,) + arrived.shape[2:])

    def fetch(positions):
        return jnp.einsum(
            "gq,qcbn->gcbn", pick_rows(positions), arrived, preferred_element_type=jnp.float32
        ).astype(jnp.bfloat16)

    weights = time_weights[0, 0]
    spread = amplitudes[0, 0]

    def add_group(index, total):
        start = index * group_slots
        positions = lax.dynamic_slice_in_dim(source_slot, start, group_slots, 0)
        blocks = fetch(positions)
        part_weights = lax.dynamic_slice_in_dim(weights, start, group_slots, 0)
        part_spread = lax.dynamic_slice_in_dim(spread, start, group_slots, 0)
        alive = (start + jnp.arange(group_slots) < own_fill).astype(jnp.float32)
        interp = jnp.einsum(
            "gtn,gcbn->gcbt", part_weights, blocks, preferred_element_type=jnp.float32
        )
        interp = (interp * alive[:, None, None, None]).astype(jnp.bfloat16)
        return total + jnp.einsum(
            "gcbt,gcbp->tp", interp, part_spread, preferred_element_type=jnp.float32
        )

    rounds = (own_fill + group_slots - 1) // group_slots
    partial_value = lax.fori_loop(
        0, rounds, add_group, jnp.zeros((weights.shape[1], spread.shape[-1]), jnp.float32)
    )
    image = lax.psum_scatter(partial_value, "trace", scatter_dimension=0, tiled=True)
    return image[None]


def per_device(traces, taps, aperture, counts, time_weights, amplitudes):
    tiles = lax.axis_size("tile")
    every_block = traces.shape[1] * tiles
    gathers = every_block == aperture.shape[2] and tiles % 4 == 0
    form = gather_per_device if gathers else exchange_per_device
    return form(traces, taps, aperture, counts, time_weights, amplitudes)


def solution(mesh):
    placed = (
        P("trace", "tile", None, None),
        P(),
        P("trace", None, None),
        P("trace", None),
        P("trace", "tile", None, None, None),
        P("trace", "tile", None, None, None, None),
    )
    return jax.shard_map(
        per_device, mesh=mesh, in_specs=placed, out_specs=P("tile", "trace", None), check_vma=False
    )
```

```python
import functools

import jax
import jax.numpy as jnp
from jax import lax
from jax.experimental import pallas as pl
from jax.experimental.pallas import tpu as pltpu
from jax.sharding import PartitionSpec as P

group_slots = 8
lane_group = 4
halves = 2
pieces = 2
MESH = pl.DeviceIdType.MESH


def migrate_kernel(
    rows_z,
    subsets,
    counts_hbm,
    aperture_hbm,
    taps_hbm,
    traces_ref,
    weights_ref,
    spread_ref,
    out_ref,
    gathered,
    weights,
    spread,
    operator,
    filtered,
    total,
    parts,
    counts_ref,
    aperture_ref,
    taps_ref,
    band,
    lookup,
    slot_of,
    recv_sem,
    send_z_sem,
    send_x_sem,
    load_sem,
    part_send_sem,
    part_recv_sem,
):
    tile = lax.axis_index("tile")
    subset = lax.axis_index("trace")
    z = tile // 2
    x = tile % 2
    other = 1 - x
    samples = operator.shape[1]
    chunk_rows = gathered.shape[2]
    block_rows = spread.shape[2]
    chunk_blocks = chunk_rows // block_rows
    block_count = chunk_blocks * halves
    group_lanes = lane_group * block_rows

    load_small = [
        pltpu.make_async_copy(src, dst, load_sem.at[4 + at])
        for at, (src, dst) in enumerate(
            ((counts_hbm, counts_ref), (aperture_hbm, aperture_ref), (taps_hbm, taps_ref))
        )
    ]
    load_own = pltpu.make_async_copy(traces_ref, gathered.at[tile], load_sem.at[0])
    load_weights = pltpu.make_async_copy(weights_ref, weights, load_sem.at[1])
    load_spread = pltpu.make_async_copy(spread_ref, spread, load_sem.at[2])

    barrier = pltpu.get_barrier_semaphore()

    @pl.when(z > 0)
    def _():
        pl.semaphore_signal(barrier, inc=1, device_id=(tile - 2, subset), device_id_type=MESH)

    @pl.when(z < rows_z - 1)
    def _():
        pl.semaphore_signal(barrier, inc=1, device_id=(tile + 2, subset), device_id_type=MESH)

    pl.semaphore_signal(barrier, inc=1, device_id=(z * 2 + other, subset), device_id_type=MESH)
    for step in range(1, subsets):
        pl.semaphore_signal(
            barrier, inc=1, device_id=(tile, (subset + step) % subsets), device_id_type=MESH
        )
    for load in load_small:
        load.start()
    load_own.start()
    inner = jnp.where((z > 0) & (z < rows_z - 1), 1, 0)
    pl.semaphore_wait(barrier, subsets + 1 + inner)

    units = halves * pieces
    piece_rows = chunk_rows // pieces

    def place(unit):
        return unit // pieces, pl.ds((unit % pieces) * piece_rows, piece_rows)

    def source(origin_z, unit, own):
        if own:
            return traces_ref.at[place(unit)]
        return gathered.at[(origin_z * 2 + x, *place(unit))]

    def send_z(origin_z, unit, up, own=False):
        return pltpu.make_async_remote_copy(
            src_ref=source(origin_z, unit, own),
            dst_ref=gathered.at[(origin_z * 2 + x, *place(unit))],
            send_sem=send_z_sem.at[up, origin_z, unit],
            recv_sem=recv_sem.at[origin_z * 2 + x, unit],
            device_id=(tile + 4 * up - 2, subset),
            device_id_type=MESH,
        )

    def send_x(origin_z, unit, own=False):
        return pltpu.make_async_remote_copy(
            src_ref=source(origin_z, unit, own),
            dst_ref=gathered.at[(origin_z * 2 + x, *place(unit))],
            send_sem=send_x_sem.at[origin_z, unit],
            recv_sem=recv_sem.at[origin_z * 2 + x, unit],
            device_id=(z * 2 + other, subset),
            device_id_type=MESH,
        )

    def wait_arrival(origin, unit):
        pltpu.make_async_remote_copy(
            src_ref=gathered.at[(origin, *place(unit))],
            dst_ref=gathered.at[(origin, *place(unit))],
            send_sem=send_x_sem.at[0, 0],
            recv_sem=recv_sem.at[origin, unit],
            device_id=(z * 2 + other, subset),
            device_id_type=MESH,
        ).wait_recv()

    for unit in range(units):

        @pl.when(z < rows_z - 1)
        def _():
            send_z(z, unit, 1, True).start()

        @pl.when(z > 0)
        def _():
            send_z(z, unit, 0, True).start()

        send_x(z, unit, True).start()

    load_weights.start()
    load_spread.start()
    for load in load_small:
        load.wait()
    slots = weights.shape[0]
    listing = aperture_ref[0, pl.ds(tile, 1), :]
    slot = lax.broadcasted_iota(jnp.int32, (slots, slots), 0)
    block = lax.broadcasted_iota(jnp.int32, (slots, slots), 1)
    named = jnp.broadcast_to(listing, (slots, slots)).T
    match = (named == block) & (slot < counts_ref[0, tile])
    lookup[...] = jnp.broadcast_to(
        jnp.sum(jnp.where(match, slot + 1, 0), axis=0, keepdims=True) - 1, lookup.shape
    )
    publish = pltpu.make_async_copy(lookup, slot_of, load_sem.at[3])
    publish.start()

    half_taps = (taps_ref.shape[1] - 1) // 2
    band[...] = jnp.zeros_like(band)
    band[0:2, 0 : taps_ref.shape[1]] = taps_ref[...].astype(jnp.float32)
    row = lax.broadcasted_iota(jnp.int32, (samples, samples), 0)
    gap = lax.broadcasted_iota(jnp.int32, (samples, samples), 1) - row
    inside = (gap <= half_taps) & (gap >= -half_taps)
    for channel in range(2):
        centred = pltpu.roll(band[...], samples - half_taps, 1)[channel : channel + 1, :]
        shifted = jnp.broadcast_to(centred, (samples, samples))
        shift = 1
        while shift < samples:
            shifted = jnp.where((row // shift) % 2 == 1, pltpu.roll(shifted, shift, 1), shifted)
            shift *= 2
        operator[channel * samples : (channel + 1) * samples, :] = (
            jnp.where(inside, shifted, 0.0).T
        ).astype(operator.dtype)
    total[...] = jnp.zeros_like(total)

    lanes = lax.broadcasted_iota(jnp.int32, (1, 2 * group_lanes), 1)
    member = (lanes // block_rows) % lane_group

    def compute(origin, half):
        filtered[...] = lax.dot_general(
            operator[...],
            gathered[origin, half],
            (((1,), (1,)), ((), ())),
            preferred_element_type=jnp.float32,
        ).astype(filtered.dtype)
        taus = weights.shape[1]
        for group in range(chunk_blocks // lane_group):
            first = group * group_lanes
            blocks = jnp.concatenate(
                [
                    filtered[0:samples, first : first + group_lanes],
                    filtered[samples : 2 * samples, first : first + group_lanes],
                ],
                axis=1,
            )
            base = origin * block_count + half * chunk_blocks + group * lane_group
            found = [slot_of[0, base + index] for index in range(lane_group)]
            picks = [jnp.maximum(value, 0) for value in found]
            gains = [jnp.where(value >= 0, 1.0, 0.0) for value in found]
            stacked = jnp.concatenate([weights[pick] for pick in picks], axis=0)
            product = jnp.dot(stacked, blocks, preferred_element_type=jnp.float32)
            interp = product[0:taus]
            alive = jnp.full((1, 2 * group_lanes), gains[0], jnp.float32)
            for index in range(1, lane_group):
                here = member == index
                interp = jnp.where(here, product[index * taus : (index + 1) * taus], interp)
                alive = jnp.where(here, gains[index], alive)
            interp = (interp * alive).astype(jnp.bfloat16)
            columns = jnp.concatenate(
                [spread[pick, channel] for channel in range(2) for pick in picks], axis=0
            )
            total[...] += jnp.dot(interp, columns, preferred_element_type=jnp.float32)

    load_own.wait()
    load_weights.wait()
    load_spread.wait()
    publish.wait()

    def own_chunk(half, carry):
        compute(tile, half)
        return carry

    lax.fori_loop(0, halves, own_chunk, 0)

    for distance in range(1, rows_z + 1):
        for half in range(halves):
            for unit in range(half * pieces, (half + 1) * pieces):
                for up in (1, 0):
                    origin_z = z - distance if up else z + distance

                    @pl.when((origin_z >= 0) & (origin_z < rows_z))
                    def _():
                        wait_arrival(origin_z * 2 + x, unit)

                        @pl.when((z > 0) & (z < rows_z - 1))
                        def _():
                            send_z(origin_z, unit, up).start()

                        send_x(origin_z, unit).start()

            def column_chunk(event, carry):
                half = event // 2
                up = event % 2
                near = z - distance * (2 * up - 1)
                far = z - (distance - 1) * (2 * up - 1)

                @pl.when((near >= 0) & (near < rows_z))
                def _():
                    compute(near * 2 + x, half)

                wanted = (far >= 0) & (far < rows_z)
                if distance == 1:
                    wanted = up == 1

                @pl.when(wanted)
                def _():
                    for piece in range(pieces):
                        wait_arrival(far * 2 + other, half * pieces + piece)
                    compute(far * 2 + other, half)

                return carry

            lax.fori_loop(2 * half, 2 * half + 2, column_chunk, 0)

    share = out_ref.shape[0]
    sends = []
    for step in range(1, subsets):
        peer = (subset + step) % subsets
        copy = pltpu.make_async_remote_copy(
            src_ref=total.at[pl.ds(pl.multiple_of(peer * share, share), share)],
            dst_ref=parts.at[step - 1],
            send_sem=part_send_sem.at[step - 1],
            recv_sem=part_recv_sem.at[step - 1],
            device_id=(tile, peer),
            device_id_type=MESH,
        )
        copy.start()
        sends.append(copy)
    result = total[pl.ds(pl.multiple_of(subset * share, share), share), :]
    for step in range(1, subsets):
        sends[step - 1].wait_recv()
        result = result + parts[step - 1]
    out_ref[...] = result
    for copy in sends:
        copy.wait_send()

    for unit in range(units):

        @pl.when(z < rows_z - 1)
        def _():
            send_z(z, unit, 1, True).wait_send()

        @pl.when(z > 0)
        def _():
            send_z(z, unit, 0, True).wait_send()

        send_x(z, unit, True).wait_send()
        for distance in range(1, rows_z):
            for up in (1, 0):
                origin_z = z - distance if up else z + distance

                @pl.when((origin_z >= 0) & (origin_z < rows_z))
                def _():
                    @pl.when((z > 0) & (z < rows_z - 1))
                    def _():
                        send_z(origin_z, unit, up).wait_send()

                    send_x(origin_z, unit).wait_send()


def keep(array):
    return pltpu.with_memory_space_constraint(array, pltpu.HBM)


def gather_per_device(traces, taps, aperture, counts, time_weights, amplitudes):
    tiles = lax.axis_size("tile")
    subsets = lax.axis_size("trace")
    _, block_count, block_rows, samples = traces.shape
    slots, taus = time_weights.shape[2:4]
    columns = amplitudes.shape[-1]
    chunk_rows = block_count * block_rows // halves
    share = taus // subsets
    rows_z = tiles // 2
    units = halves * pieces
    vmem = pl.BlockSpec(memory_space=pltpu.VMEM)
    hbm = pl.BlockSpec(memory_space=pl.ANY)
    image = pl.pallas_call(
        functools.partial(migrate_kernel, rows_z, subsets),
        out_shape=jax.ShapeDtypeStruct((share, columns), jnp.float32),
        in_specs=[hbm] * 6,
        out_specs=vmem,
        scratch_shapes=[
            pltpu.VMEM((tiles, halves, chunk_rows, samples), jnp.bfloat16),
            pltpu.VMEM((slots, taus, samples), jnp.bfloat16),
            pltpu.VMEM((slots, 2, block_rows, columns), jnp.bfloat16),
            pltpu.VMEM((2 * samples, samples), jnp.bfloat16),
            pltpu.VMEM((2 * samples, chunk_rows), jnp.bfloat16),
            pltpu.VMEM((taus, columns), jnp.float32),
            pltpu.VMEM((subsets - 1, share, columns), jnp.float32),
            pltpu.SMEM(counts.shape, jnp.int32),
            pltpu.VMEM(aperture.shape, jnp.int32),
            pltpu.VMEM(taps.shape, taps.dtype),
            pltpu.VMEM((8, samples), jnp.float32),
            pltpu.VMEM((8, slots), jnp.int32),
            pltpu.SMEM((8, slots), jnp.int32),
            pltpu.SemaphoreType.DMA((tiles, units)),
            pltpu.SemaphoreType.DMA((2, rows_z, units)),
            pltpu.SemaphoreType.DMA((rows_z, units)),
            pltpu.SemaphoreType.DMA((7,)),
            pltpu.SemaphoreType.DMA((subsets - 1,)),
            pltpu.SemaphoreType.DMA((subsets - 1,)),
        ],
        compiler_params=pltpu.CompilerParams(
            collective_id=0, has_side_effects=True, vmem_limit_bytes=48 * 1024 * 1024
        ),
    )(
        keep(counts),
        keep(aperture),
        keep(taps),
        keep(traces.reshape(halves, chunk_rows, samples)),
        keep(time_weights[0, 0]),
        keep(amplitudes[0, 0]),
    )
    return image[None]


def filter_matrix(taps, samples):
    width = taps.shape[1]
    center = (width - 1) // 2
    offset = jnp.arange(samples)[:, None] - jnp.arange(samples)[None, :] + center
    table = (offset[:, :, None] == jnp.arange(width)[None, None, :]).astype(jnp.bfloat16)
    return jnp.einsum("ct,nmt->cnm", taps, table, preferred_element_type=jnp.float32).astype(
        jnp.bfloat16
    )


def exchange_per_device(traces, taps, aperture, counts, time_weights, amplitudes):
    tiles = lax.axis_size("tile")
    myself = lax.axis_index("tile")
    block_count = traces.shape[1]
    samples = traces.shape[3]
    slots = aperture.shape[2]
    capacity = max(2, slots // tiles)
    listing = aperture[0]
    filled = counts[0]
    owners = listing // block_count
    within = listing - owners * block_count
    order = jnp.arange(slots)
    earlier = order[None, :] < order[:, None]
    rank = jnp.sum((owners[:, :, None] == owners[:, None, :]) & earlier[None], axis=2)
    alive_slots = order[None, :] < filled[:, None]
    mine = (owners == myself) & alive_slots
    rank_onehot = (
        (rank[:, :, None] == jnp.arange(capacity)[None, None, :]) & mine[:, :, None]
    ).astype(jnp.bfloat16)
    local_onehot = (within[:, :, None] == jnp.arange(block_count)[None, None, :]).astype(
        jnp.bfloat16
    )
    select = jnp.einsum(
        "ksc,ksl->kcl", rank_onehot, local_onehot, preferred_element_type=jnp.float32
    ).astype(jnp.bfloat16)
    operator = filter_matrix(taps, samples)
    own_owner = lax.dynamic_index_in_dim(owners, myself, 0, keepdims=False)
    own_rank = lax.dynamic_index_in_dim(rank, myself, 0, keepdims=False)
    own_fill = lax.dynamic_index_in_dim(filled, myself, 0, keepdims=False)
    source_slot = own_owner * capacity + own_rank
    arrived_rows = tiles * capacity

    def pick_rows(positions):
        return (positions[:, None] == jnp.arange(arrived_rows)[None, :]).astype(jnp.bfloat16)

    filtered = jnp.einsum(
        "cnm,kbm->kcbn", operator, traces[0], preferred_element_type=jnp.float32
    ).astype(jnp.bfloat16)
    outgoing = jnp.einsum(
        "kcl,lqbn->kcqbn", select, filtered, preferred_element_type=jnp.float32
    ).astype(jnp.bfloat16)
    arrived = lax.all_to_all(outgoing, "tile", split_axis=0, concat_axis=0, tiled=True)
    arrived = arrived.reshape((arrived_rows,) + arrived.shape[2:])

    def fetch(positions):
        return jnp.einsum(
            "gq,qcbn->gcbn", pick_rows(positions), arrived, preferred_element_type=jnp.float32
        ).astype(jnp.bfloat16)

    weights = time_weights[0, 0]
    spread = amplitudes[0, 0]

    def add_group(index, total):
        start = index * group_slots
        positions = lax.dynamic_slice_in_dim(source_slot, start, group_slots, 0)
        blocks = fetch(positions)
        part_weights = lax.dynamic_slice_in_dim(weights, start, group_slots, 0)
        part_spread = lax.dynamic_slice_in_dim(spread, start, group_slots, 0)
        alive = (start + jnp.arange(group_slots) < own_fill).astype(jnp.float32)
        interp = jnp.einsum(
            "gtn,gcbn->gcbt", part_weights, blocks, preferred_element_type=jnp.float32
        )
        interp = (interp * alive[:, None, None, None]).astype(jnp.bfloat16)
        return total + jnp.einsum(
            "gcbt,gcbp->tp", interp, part_spread, preferred_element_type=jnp.float32
        )

    rounds = (own_fill + group_slots - 1) // group_slots
    partial_value = lax.fori_loop(
        0, rounds, add_group, jnp.zeros((weights.shape[1], spread.shape[-1]), jnp.float32)
    )
    image = lax.psum_scatter(partial_value, "trace", scatter_dimension=0, tiled=True)
    return image[None]


def per_device(traces, taps, aperture, counts, time_weights, amplitudes):
    tiles = lax.axis_size("tile")
    every_block = traces.shape[1] * tiles
    gathers = every_block == aperture.shape[2] and tiles % 4 == 0
    form = gather_per_device if gathers else exchange_per_device
    return form(traces, taps, aperture, counts, time_weights, amplitudes)


def solution(mesh):
    placed = (
        P("trace", "tile", None, None),
        P(),
        P("trace", None, None),
        P("trace", None),
        P("trace", "tile", None, None, None),
        P("trace", "tile", None, None, None, None),
    )
    return jax.shard_map(
        per_device, mesh=mesh, in_specs=placed, out_specs=P("tile", "trace", None), check_vma=False
    )
```
